32 devices in a mesh: snp: 8 (over z, x), trait: 4 (over y, core).
Axes of the slice: x: 2, y: 2, z: 4, core: 2. Of those that a mesh axis runs over, the one named last changes fastest.
Arguments:
- genotype: bfloat16 [32, 8192], P(None, 'snp'), may hold values from -0.0625 to 0.0625
- targets: bfloat16 [32, 16384], P('snp', 'trait'), may hold values from -6 to 6
- effect_sizes: float32 [8192, 16384], P('snp', 'trait'), may hold values from -6 to 6
- membership: int32 [4, 128, 128], replicated, may hold values from 0 to 1, as said below
- node_weight: float32 [4, 128], replicated, may hold values from 0.03 to 1
Outputs:
- updated: float32 [8192, 16384], P('snp', 'trait')
The draws below stay inside these ranges and needn't reach their ends.
Inputs may be any that keep to these rules, and one draw needn't show every extreme that they name: `membership`: at each level the node slots 0 .. c - 1 partition all 128 trait blocks, the remaining slots cover none; every node of a level lies inside one node of the next level; at level 0 each block is its own node.
All inputs are finite; a program needn't handle non-finite values.
Results may differ from the reference program's by a relative error of at most 0.00042.
Values may be sent and summed in bfloat16 or wider, within the bound.
A program may use at most 128 MiB of HBM per device.

```python
import math
import jax
import jax.numpy as jnp
from jax import lax

J = 8192
TB = 128
BLOCKS = 128
LEVELS = 4
ITERS = 1
K = 16384
NODES = 128
N = 32


def draw_membership(key, part):
    order = jax.random.permutation(jax.random.fold_in(key, 1), BLOCKS)
    boundary = jnp.ones((BLOCKS,), jnp.int32)
    first = (jnp.arange(BLOCKS) == 0).astype(jnp.int32)
    slots = jnp.arange(BLOCKS, dtype=jnp.int32)
    levels_out = []
    for level in range(LEVELS):
        if level > 0:
            coin = jax.random.randint(jax.random.fold_in(key, 10 + level), (BLOCKS,), 0, 2)
            boundary = jnp.maximum(boundary * (coin == 0).astype(jnp.int32), first)
        node_pos = (jnp.cumsum(boundary) - 1).astype(jnp.int32)
        node_block = jnp.zeros((BLOCKS,), jnp.int32).at[order].set(node_pos)
        levels_out.append((slots[:, None] == node_block[None, :]).astype(jnp.int32))
    return jnp.stack(levels_out, axis=0)


def level_of(key, dims, cuts, smallest, largest):
    gain, own = 1.0, jax.random.fold_in(key, 6)
    for position, blocks in cuts:
        draws = jnp.exp(jax.random.uniform(jax.random.fold_in(own, position), (blocks,), jnp.float32, smallest / len(cuts), largest / len(cuts)))
        gain = gain * jnp.repeat(draws, dims[position] // blocks).reshape([-1 if axis == position else 1 for axis in range(len(dims))])
    return gain


def gaussian(stream_key, shape, width, most, shards=(), kind=jnp.bfloat16):
    loudness = level_of(stream_key, shape, shards, -0.22, 0.18) if shards else 1.0
    entries = jax.random.normal(stream_key, shape, jnp.float32) * width * loudness
    return jnp.minimum(jnp.maximum(entries, -most), most).astype(kind)


def setup_inputs(seed: int = 0) -> dict:
    key_list = jax.random.split(jax.random.key(seed), 6)
    return {
        "genotype": gaussian(key_list[0], (N, J), J ** -0.5, 0.0625, ((1, 8),)),
        "targets": gaussian(key_list[1], (N, K), 1.0, 6.0, ((0, 8), (1, 4))),
        "effect_sizes": gaussian(key_list[2], (J, K), 1.0, 6.0, ((0, 8), (1, 4)), jnp.float32),
        "membership": draw_membership(jax.random.fold_in(key_list[5], 71), 0),
        "node_weight": jnp.clip(jnp.exp(jax.random.uniform(key_list[4], (LEVELS, NODES), jnp.float32, math.log(0.03), math.log(1.0))), 0.03, 1.0),
    }


step_size = 0.5

def shrink_tree(value, membership, node_weight):
    for level in range(LEVELS):
        member = membership[level].astype(jnp.float32)
        count = lax.optimization_barrier(jnp.sum(member, axis=1))
        threshold = step_size * node_weight[level] * jnp.sqrt(TB * jnp.maximum(count, 1.0))
        blocks = value.reshape(value.shape[0], BLOCKS, TB)
        block_sq = lax.optimization_barrier(jnp.sum(blocks * blocks, axis=2))
        node_sq = jnp.dot(block_sq, member.T, precision=lax.Precision.HIGHEST)
        norm = jnp.sqrt(node_sq)
        factor = jnp.maximum(norm - threshold, 0.0) / jnp.maximum(norm, threshold)
        block_factor = jnp.dot(factor, member, precision=lax.Precision.HIGHEST)
        value = (blocks * block_factor[:, :, None]).reshape(value.shape)
    return value

def reference(genotype, targets, effect_sizes, membership, node_weight):
    current = effect_sizes
    for sweep_index in range(ITERS):
        current_bf = current.astype(jnp.bfloat16)
        fitted = jnp.dot(genotype, current_bf, preferred_element_type=jnp.float32)
        residual = (targets.astype(jnp.float32) - fitted).astype(jnp.bfloat16)
        gradient = lax.dot_general(genotype, residual, (((0,), (0,)), ((), ())), preferred_element_type=jnp.float32)
        current = shrink_tree(current + step_size * gradient, membership, node_weight)
    return current
```

```python
import functools

import jax
import jax.numpy as jnp
from jax import lax
from jax.experimental import pallas as pl
from jax.experimental.pallas import tpu as pltpu
from jax.sharding import PartitionSpec as P

TB = 128
SUB = 8
STEP = 0.5
F32 = jnp.float32
BF16 = jnp.bfloat16
WIRE = jnp.float32
MESH = pl.DeviceIdType.MESH
HIGH = lax.Precision.HIGHEST
NT = (((1,), (1,)), ((), ()))
TN = (((0,), (0,)), ((), ()))


def one_hot_rows(rows, samples, per, half):
    r = lax.broadcasted_iota(jnp.int32, (rows, samples), 0)
    n = lax.broadcasted_iota(jnp.int32, (rows, samples), 1)
    owner = lax.shift_right_logical(r, 3)
    inner = jnp.bitwise_and(r, 7) - half * per
    hit = (n == owner * per + inner) & (inner >= 0) & (inner < per)
    return jnp.where(hit, 1.0, 0.0).astype(BF16)


def fit_kernel(
    n, trait, chunks, row_tile,
    g_ref, t_ref, m_ref, w_ref, e_hbm,
    v_ref, sc_ref,
    send, got, res, rg, gs, gt, bq, bt, gq, so, si, ssum, thr,
    e_sem, rs_send, rs_recv, ag_send, ag_recv, x_send, x_recv, y_send, y_recv,
):
    me = lax.axis_index("snp")
    mt = lax.axis_index("trait")
    samples, rows = g_ref.shape
    per = samples // n
    halves = SUB // per
    cols = v_ref.shape[1]
    half = cols // halves
    w = half // chunks
    blocks = cols // TB
    levels = m_ref.shape[0]
    q = rows // trait

    def col(h, c):
        return pl.ds(pl.multiple_of(h * half + c * w, w), w)

    def part(c):
        return pl.ds(pl.multiple_of(c * w, w), w)

    def load(h, c):
        return pltpu.make_async_copy(
            e_hbm.at[:, col(h, c)], v_ref.at[:, col(h, c)], e_sem.at[c, h]
        )

    for c in range(chunks):
        for h in range(halves):
            load(h, c).start()

    barrier = pltpu.get_barrier_semaphore()

    def greet_snp(k, _):
        pl.semaphore_signal(
            barrier, inc=1, device_id={"snp": lax.rem(me + k, n)}, device_id_type=MESH
        )
        return 0

    def greet_trait(k, _):
        pl.semaphore_signal(
            barrier, inc=1, device_id={"trait": lax.rem(mt + k, trait)}, device_id_type=MESH
        )
        return 0

    lax.fori_loop(1, n, greet_snp, 0)
    lax.fori_loop(1, trait, greet_trait, 0)

    for h in range(halves):
        pick = one_hot_rows(n * SUB, samples, per, h)
        gs[h] = jnp.dot(pick, g_ref[...], preferred_element_type=F32).astype(BF16)
        gt[h] = lax.dot_general(
            g_ref[...], pick, (((0,), (1,)), ((), ())), preferred_element_type=F32
        ).astype(BF16)

    pl.semaphore_wait(barrier, n + trait - 2)

    def rs_copy(c, to, frm):
        return pltpu.make_async_remote_copy(
            src_ref=send.at[to, :, part(c)],
            dst_ref=got.at[frm, :, part(c)],
            send_sem=rs_send.at[c, to],
            recv_sem=rs_recv.at[c, frm],
            device_id={"snp": to},
            device_id_type=MESH,
        )

    def ag_copy(c, to, frm):
        return pltpu.make_async_remote_copy(
            src_ref=res.at[:, part(c)],
            dst_ref=rg.at[frm, :, part(c)],
            send_sem=ag_send.at[c, to],
            recv_sem=ag_recv.at[c, frm],
            device_id={"snp": to},
            device_id_type=MESH,
        )

    def x_copy(to, frm):
        return pltpu.make_async_remote_copy(
            src_ref=bt.at[to],
            dst_ref=gq.at[frm],
            send_sem=x_send.at[to],
            recv_sem=x_recv.at[frm],
            device_id={"trait": to},
            device_id_type=MESH,
        )

    def y_copy(to, frm):
        return pltpu.make_async_remote_copy(
            src_ref=so.at[to],
            dst_ref=si.at[frm],
            send_sem=y_send.at[to],
            recv_sem=y_recv.at[frm],
            device_id={"trait": to},
            device_id_type=MESH,
        )

    def peers(count, own, fn):
        def step(k, _):
            fn(lax.rem(own + k, count))
            return 0

        lax.fori_loop(1, count, step, 0)

    kt = min(rows, 256)

    def fit_chunk(c, _):
        total = jnp.zeros((n * SUB, w), F32)
        for h in range(halves):
            load(h, c).wait()
            for k in range(rows // kt):
                total += jnp.dot(
                    gs[h, :, k * kt : (k + 1) * kt],
                    v_ref[k * kt : (k + 1) * kt, col(h, c)].astype(BF16),
                    preferred_element_type=F32,
                )
        send[:, :, part(c)] = total.reshape(n, SUB, w).astype(send.dtype)
        got[me, :, part(c)] = send[me, :, part(c)]
        peers(n, me, lambda p: rs_copy(c, p, me).start())
        return 0

    lax.fori_loop(0, chunks, fit_chunk, 0)

    for level in range(levels):
        member = m_ref[level].astype(F32)
        count = jnp.sum(member, axis=1, keepdims=True)
        weight = jnp.broadcast_to(w_ref[level : level + 1, :], member.shape).T
        by_node = STEP * weight * jnp.sqrt(TB * jnp.maximum(count, 1.0))
        thr[level] = lax.dot_general(
            member, by_node, TN, precision=HIGH, preferred_element_type=F32
        )
        ssum[level] = lax.dot_general(
            member, member, TN, precision=HIGH, preferred_element_type=F32
        )

    def res_chunk(c, _):
        peers(n, me, lambda p: rs_copy(c, p, p).wait_recv())
        fitted = jnp.sum(got[:, :, part(c)].astype(F32), axis=0)
        target = jnp.concatenate(
            [t_ref[:, col(h, c)].astype(F32) for h in range(halves)], axis=0
        )
        residual = (target - fitted).astype(BF16)
        res[:, part(c)] = residual
        rg[me, :, part(c)] = residual
        peers(n, me, lambda p: ag_copy(c, p, me).start())
        return 0

    lax.fori_loop(0, chunks, res_chunk, 0)

    lane = lax.broadcasted_iota(jnp.int32, (row_tile, TB), 1)

    def value_chunk(c, _):
        peers(n, me, lambda p: ag_copy(c, p, p).wait_recv())
        resid = rg[:, :, part(c)].reshape(n * SUB, w)

        def tile(i, _):
            r = pl.ds(pl.multiple_of(i * row_tile, row_tile), row_tile)
            sums = bq[r, :]
            for h in range(halves):
                grad = jnp.dot(gt[h, r, :], resid, preferred_element_type=F32)
                value = v_ref[r, col(h, c)] + STEP * grad
                v_ref[r, col(h, c)] = value
                sq = value * value
                first = (h * half + c * w) // TB
                for b in range(w // TB):
                    s = jnp.sum(sq[:, b * TB : (b + 1) * TB], axis=1, keepdims=True)
                    sums = jnp.where(lane == first + b, s, sums)
            bq[r, :] = sums
            return 0

        lax.fori_loop(0, rows // row_tile, tile, 0)
        return 0

    bq[...] = jnp.zeros_like(bq)
    lax.fori_loop(0, chunks, value_chunk, 0)

    for k in range(trait):
        bt[k] = bq[k * q : (k + 1) * q, :].T[:blocks]
    peers(trait, mt, lambda p: x_copy(p, mt).start())
    gq[mt] = bt[mt]
    peers(trait, mt, lambda p: x_copy(p, p).wait_recv())

    block_sq = gq[...].reshape(trait * blocks, q)
    scale = None
    for level in range(levels):
        if level == 0:
            node_sq = block_sq
        else:
            node_sq = jnp.dot(
                ssum[level], block_sq, precision=HIGH, preferred_element_type=F32
            )
        norm = jnp.sqrt(node_sq)
        limit = thr[level][:, :1]
        factor = jnp.maximum(norm - limit, 0.0) / jnp.maximum(norm, limit)
        scale = factor if scale is None else scale * factor
        block_sq = block_sq * (factor * factor)
    so[...] = scale.reshape(trait, blocks, q)
    peers(trait, mt, lambda p: y_copy(p, mt).start())
    si[mt] = so[mt]
    peers(trait, mt, lambda p: y_copy(p, p).wait_recv())
    for k in range(trait):
        sc_ref[k * q : (k + 1) * q, :blocks] = si[k].T

    def drain(c, _):
        peers(n, me, lambda p: rs_copy(c, p, me).wait_send())
        peers(n, me, lambda p: ag_copy(c, p, me).wait_send())
        return 0

    lax.fori_loop(0, chunks, drain, 0)
    peers(trait, mt, lambda p: x_copy(p, mt).wait_send())
    peers(trait, mt, lambda p: y_copy(p, mt).wait_send())


def scale_kernel(pieces, row_tile, v_ref, sc_ref, o_hbm, out, sem):
    rows, cols = v_ref.shape
    size = rows // pieces

    def store(p):
        r = pl.ds(pl.multiple_of(p * size, size), size)
        return pltpu.make_async_copy(out.at[r, :], o_hbm.at[r, :], sem.at[p])

    def piece(p, _):
        def tile(i, _):
            start = pl.multiple_of(p * size + i * row_tile, row_tile)
            r = pl.ds(start, row_tile)
            sc = sc_ref[r, :]
            for b in range(cols // TB):
                c = slice(b * TB, (b + 1) * TB)
                out[r, c] = v_ref[r, c] * sc[:, b : b + 1]
            return 0

        lax.fori_loop(0, size // row_tile, tile, 0)
        store(p).start()
        return 0

    lax.fori_loop(0, pieces, piece, 0)
    lax.fori_loop(0, pieces, lambda p, _: (store(p).wait(), 0)[1], 0)


def body(n, trait, genotype, targets, effect_sizes, membership, node_weight):
    samples, rows = genotype.shape
    cols = effect_sizes.shape[1]
    blocks = cols // TB
    levels, nodes, _ = membership.shape
    halves = SUB // (samples // n)
    half = cols // halves
    chunks = 4
    q = rows // trait
    vmem = pl.BlockSpec(memory_space=pltpu.VMEM)
    hbm = pl.BlockSpec(memory_space=pl.ANY)
    dma = pltpu.SemaphoreType.DMA
    value, scale = pl.pallas_call(
        functools.partial(fit_kernel, n, trait, chunks, min(rows, 64)),
        name="fit",
        out_shape=(pltpu.VMEM((rows, cols), F32), pltpu.VMEM((rows, TB), F32)),
        in_specs=[vmem] * 4 + [hbm],
        out_specs=(vmem, vmem),
        scratch_shapes=[
            pltpu.VMEM((n, SUB, half), WIRE),
            pltpu.VMEM((n, SUB, half), WIRE),
            pltpu.VMEM((SUB, half), BF16),
            pltpu.VMEM((n, SUB, half), BF16),
            pltpu.VMEM((halves, n * SUB, rows), BF16),
            pltpu.VMEM((halves, rows, n * SUB), BF16),
            pltpu.VMEM((rows, TB), F32),
            pltpu.VMEM((trait, blocks, q), F32),
            pltpu.VMEM((trait, blocks, q), F32),
            pltpu.VMEM((trait, blocks, q), F32),
            pltpu.VMEM((trait, blocks, q), F32),
            pltpu.VMEM((levels, nodes, nodes), F32),
            pltpu.VMEM((levels, nodes, nodes), F32),
            dma((chunks, halves)),
            dma((chunks, n)),
            dma((chunks, n)),
            dma((chunks, n)),
            dma((chunks, n)),
            dma((trait,)),
            dma((trait,)),
            dma((trait,)),
            dma((trait,)),
        ],
        compiler_params=pltpu.CompilerParams(
            collective_id=0, has_side_effects=True, vmem_limit_bytes=40 << 20
        ),
    )(genotype, targets, membership, node_weight, effect_sizes)
    pieces = 8
    return pl.pallas_call(
        functools.partial(scale_kernel, pieces, min(rows // pieces, 32)),
        name="scale",
        out_shape=jax.ShapeDtypeStruct((rows, cols), F32),
        in_specs=[vmem, vmem],
        out_specs=hbm,
        scratch_shapes=[pltpu.VMEM((rows, cols), F32), dma((pieces,))],
        compiler_params=pltpu.CompilerParams(vmem_limit_bytes=40 << 20),
    )(value, scale)


def solution(mesh):
    n, trait = mesh.shape["snp"], mesh.shape["trait"]
    return jax.shard_map(
        functools.partial(body, n, trait),
        mesh=mesh,
        in_specs=(P(None, "snp"), P("snp", "trait"), P("snp", "trait"), P(), P()),
        out_specs=P("snp", "trait"),
        check_vma=False,
    )
```

```python
import functools

import jax
import jax.numpy as jnp
from jax import lax
from jax.experimental import pallas as pl
from jax.experimental.pallas import tpu as pltpu
from jax.sharding import PartitionSpec as P

TB = 128
SUB = 8
STEP = 0.5
F32 = jnp.float32
BF16 = jnp.bfloat16
LAG = 2
MESH = pl.DeviceIdType.MESH
HIGH = lax.Precision.HIGHEST
NT = (((1,), (1,)), ((), ()))
TN = (((0,), (0,)), ((), ()))


def aligned(x, m):
    return x if isinstance(x, int) else pl.multiple_of(x, m)


def one_hot_rows(rows, samples, per, half):
    r = lax.broadcasted_iota(jnp.int32, (rows, samples), 0)
    n = lax.broadcasted_iota(jnp.int32, (rows, samples), 1)
    slot = lax.shift_right_logical(r, 3)
    line = rows // SUB // 2
    owner = jnp.where(slot < line, 2 * slot, 2 * (slot - line) + 1)
    inner = jnp.bitwise_and(r, 7) - half * per
    hit = (n == owner * per + inner) & (inner >= 0) & (inner < per)
    return jnp.where(hit, 1.0, 0.0).astype(BF16)


def fit_kernel(
    n, trait, chunks, row_tile,
    g_ref, t_ref, m_ref, w_ref, e_hbm,
    v_ref, sc_ref,
    send, near, both, got, res, rg, gs, gt, bq, bt, gq, so, si, ssum, thr,
    e_sem, p_send, p_recv, rs_send, rs_recv, ag_send, ag_recv, b_send, b_recv, x_send, x_recv, y_send, y_recv,
):
    me = lax.axis_index("snp")
    mt = lax.axis_index("trait")
    mp = lax.rem(me, 2)
    mz = me // 2
    nz = n // 2
    samples, rows = g_ref.shape
    per = samples // n
    halves = SUB // per
    cols = v_ref.shape[1]
    half = cols // halves
    w = half // chunks
    blocks = cols // TB
    levels = m_ref.shape[0]
    q = rows // trait

    def col(h, c):
        return pl.ds(aligned(h * half + c * w, w), w)

    def part(c):
        return pl.ds(aligned(c * w, w), w)

    def load(h, c):
        return pltpu.make_async_copy(
            e_hbm.at[:, col(h, c)], v_ref.at[:, col(h, c)], e_sem.at[c, h]
        )

    for c in range(chunks):
        for h in range(halves):
            load(h, c).start()

    barrier = pltpu.get_barrier_semaphore()

    def greet(to):
        pl.semaphore_signal(barrier, inc=1, device_id=to, device_id_type=MESH)

    def greet_snp(k, _):
        greet({"snp": 2 * lax.rem(mz + k, nz) + mp})
        return 0

    def greet_trait(k, _):
        greet({"trait": lax.rem(mt + k, trait)})
        return 0

    greet({"snp": me + 1 - 2 * mp})
    lax.fori_loop(1, nz, greet_snp, 0)
    lax.fori_loop(1, trait, greet_trait, 0)

    for h in range(halves):
        pick = one_hot_rows(n * SUB, samples, per, h)
        gs[h] = jnp.dot(pick, g_ref[...], preferred_element_type=F32).astype(BF16)
        gt[h] = lax.dot_general(
            g_ref[...], pick, (((0,), (1,)), ((), ())), preferred_element_type=F32
        ).astype(BF16)

    pl.semaphore_wait(barrier, nz + trait - 1)

    def pair_copy(c):
        return pltpu.make_async_remote_copy(
            src_ref=send.at[1 - mp, :, :, part(c)],
            dst_ref=near.at[:, :, part(c)],
            send_sem=p_send.at[c],
            recv_sem=p_recv.at[c],
            device_id={"snp": me + 1 - 2 * mp},
            device_id_type=MESH,
        )

    def rs_copy(c, to, frm):
        return pltpu.make_async_remote_copy(
            src_ref=both.at[to, :, part(c)],
            dst_ref=got.at[frm, :, part(c)],
            send_sem=rs_send.at[c, to],
            recv_sem=rs_recv.at[c, frm],
            device_id={"snp": 2 * to + mp},
            device_id_type=MESH,
        )

    def ag_copy(c, to, frm):
        return pltpu.make_async_remote_copy(
            src_ref=res.at[:, part(c)],
            dst_ref=rg.at[mp, frm, :, part(c)],
            send_sem=ag_send.at[c, to],
            recv_sem=ag_recv.at[c, frm],
            device_id={"snp": 2 * to + mp},
            device_id_type=MESH,
        )

    def back_copy(c, parity):
        return pltpu.make_async_remote_copy(
            src_ref=rg.at[parity, :, :, part(c)],
            dst_ref=rg.at[parity, :, :, part(c)],
            send_sem=b_send.at[c],
            recv_sem=b_recv.at[c],
            device_id={"snp": me + 1 - 2 * mp},
            device_id_type=MESH,
        )

    def x_copy(to, frm):
        return pltpu.make_async_remote_copy(
            src_ref=bt.at[to],
            dst_ref=gq.at[frm],
            send_sem=x_send.at[to],
            recv_sem=x_recv.at[frm],
            device_id={"trait": to},
            device_id_type=MESH,
        )

    def y_copy(to, frm):
        return pltpu.make_async_remote_copy(
            src_ref=so.at[to],
            dst_ref=si.at[frm],
            send_sem=y_send.at[to],
            recv_sem=y_recv.at[frm],
            device_id={"trait": to},
            device_id_type=MESH,
        )

    def peers(count, own, fn):
        def step(k, _):
            fn(lax.rem(own + k, count))
            return 0

        lax.fori_loop(1, count, step, 0)

    kt = min(rows, 256)

    def fit_chunk(c, _):
        total = jnp.zeros((n * SUB, w), F32)
        for h in range(halves):
            load(h, c).wait()
            for k in range(rows // kt):
                total += jnp.dot(
                    gs[h, :, k * kt : (k + 1) * kt],
                    v_ref[k * kt : (k + 1) * kt, col(h, c)].astype(BF16),
                    preferred_element_type=F32,
                )
        send[:, :, :, part(c)] = total.reshape(2, nz, SUB, w)
        pair_copy(c).start()
        return 0

    def pair_chunk(c, _):
        pair_copy(c).wait_recv()
        both[:, :, part(c)] = send[mp, :, :, part(c)] + near[:, :, part(c)]
        peers(nz, mz, lambda p: rs_copy(c, p, mz).start())
        got[mz, :, part(c)] = both[mz, :, part(c)]
        return 0

    for c in range(chunks + LAG):
        if c < chunks:
            fit_chunk(c, 0)
        if c >= LAG:
            pair_chunk(c - LAG, 0)

    for level in range(levels):
        member = m_ref[level].astype(F32)
        count = jnp.sum(member, axis=1, keepdims=True)
        weight = jnp.broadcast_to(w_ref[level : level + 1, :], member.shape).T
        by_node = STEP * weight * jnp.sqrt(TB * jnp.maximum(count, 1.0))
        thr[level] = lax.dot_general(
            member, by_node, TN, precision=HIGH, preferred_element_type=F32
        )
        ssum[level] = lax.dot_general(
            member, member, TN, precision=HIGH, preferred_element_type=F32
        )

    def res_chunk(c):
        peers(nz, mz, lambda p: rs_copy(c, p, p).wait_recv())
        fitted = jnp.sum(got[:, :, part(c)], axis=0)
        target = jnp.concatenate(
            [t_ref[:, col(h, c)].astype(F32) for h in range(halves)], axis=0
        )
        residual = (target - fitted).astype(BF16)
        res[:, part(c)] = residual
        rg[mp, mz, :, part(c)] = residual
        peers(nz, mz, lambda p: ag_copy(c, p, mz).start())

    def back_chunk(c):
        peers(nz, mz, lambda p: ag_copy(c, p, p).wait_recv())
        back_copy(c, mp).start()

    lane = lax.broadcasted_iota(jnp.int32, (row_tile, TB), 1)

    def value_chunk(c, _):
        back_copy(c, 1 - mp).wait_recv()
        resid = rg[:, :, :, part(c)].reshape(n * SUB, w)

        def tile(i, _):
            r = pl.ds(pl.multiple_of(i * row_tile, row_tile), row_tile)
            sums = bq[r, :]
            for h in range(halves):
                grad = jnp.dot(gt[h, r, :], resid, preferred_element_type=F32)
                value = v_ref[r, col(h, c)] + STEP * grad
                v_ref[r, col(h, c)] = value
                sq = value * value
                first = (h * half + c * w) // TB
                for b in range(w // TB):
                    s = jnp.sum(sq[:, b * TB : (b + 1) * TB], axis=1, keepdims=True)
                    sums = jnp.where(lane == first + b, s, sums)
            bq[r, :] = sums
            return 0

        lax.fori_loop(0, rows // row_tile, tile, 0)
        return 0

    bq[...] = jnp.zeros_like(bq)
    for c in range(chunks + 1):
        if c < chunks:
            res_chunk(c)
        if c >= 1:
            back_chunk(c - 1)
    lax.fori_loop(0, chunks, value_chunk, 0)

    for k in range(trait):
        bt[k] = bq[k * q : (k + 1) * q, :].T[:blocks]
    peers(trait, mt, lambda p: x_copy(p, mt).start())
    gq[mt] = bt[mt]
    peers(trait, mt, lambda p: x_copy(p, p).wait_recv())

    block_sq = gq[...].reshape(trait * blocks, q)
    scale = None
    for level in range(levels):
        if level == 0:
            node_sq = block_sq
        else:
            node_sq = jnp.dot(
                ssum[level], block_sq, precision=HIGH, preferred_element_type=F32
            )
        norm = jnp.sqrt(node_sq)
        limit = thr[level][:, :1]
        factor = jnp.maximum(norm - limit, 0.0) / jnp.maximum(norm, limit)
        scale = factor if scale is None else scale * factor
        block_sq = block_sq * (factor * factor)
    so[...] = scale.reshape(trait, blocks, q)
    peers(trait, mt, lambda p: y_copy(p, mt).start())
    si[mt] = so[mt]
    peers(trait, mt, lambda p: y_copy(p, p).wait_recv())
    for k in range(trait):
        sc_ref[k * q : (k + 1) * q, :blocks] = si[k].T

    def drain(c, _):
        pair_copy(c).wait_send()
        peers(nz, mz, lambda p: rs_copy(c, p, mz).wait_send())
        peers(nz, mz, lambda p: ag_copy(c, p, mz).wait_send())
        back_copy(c, mp).wait_send()
        return 0

    lax.fori_loop(0, chunks, drain, 0)
    peers(trait, mt, lambda p: x_copy(p, mt).wait_send())
    peers(trait, mt, lambda p: y_copy(p, mt).wait_send())


def scale_kernel(pieces, row_tile, v_ref, sc_ref, o_hbm, out, sem):
    rows, cols = v_ref.shape
    size = rows // pieces

    def store(p):
        r = pl.ds(pl.multiple_of(p * size, size), size)
        return pltpu.make_async_copy(out.at[r, :], o_hbm.at[r, :], sem.at[p])

    def piece(p, _):
        def tile(i, _):
            start = pl.multiple_of(p * size + i * row_tile, row_tile)
            r = pl.ds(start, row_tile)
            sc = sc_ref[r, :]
            for b in range(cols // TB):
                c = slice(b * TB, (b + 1) * TB)
                out[r, c] = v_ref[r, c] * sc[:, b : b + 1]
            return 0

        lax.fori_loop(0, size // row_tile, tile, 0)
        store(p).start()
        return 0

    lax.fori_loop(0, pieces, piece, 0)
    lax.fori_loop(0, pieces, lambda p, _: (store(p).wait(), 0)[1], 0)


def body(n, trait, genotype, targets, effect_sizes, membership, node_weight):
    samples, rows = genotype.shape
    cols = effect_sizes.shape[1]
    blocks = cols // TB
    levels, nodes, _ = membership.shape
    halves = SUB // (samples // n)
    half = cols // halves
    chunks = 4
    nz = n // 2
    q = rows // trait
    vmem = pl.BlockSpec(memory_space=pltpu.VMEM)
    hbm = pl.BlockSpec(memory_space=pl.ANY)
    dma = pltpu.SemaphoreType.DMA
    value, scale = pl.pallas_call(
        functools.partial(fit_kernel, n, trait, chunks, min(rows, 512)),
        name="fit",
        out_shape=(pltpu.VMEM((rows, cols), F32), pltpu.VMEM((rows, TB), F32)),
        in_specs=[vmem] * 4 + [hbm],
        out_specs=(vmem, vmem),
        scratch_shapes=[
            pltpu.VMEM((2, nz, SUB, half), F32),
            pltpu.VMEM((nz, SUB, half), F32),
            pltpu.VMEM((nz, SUB, half), F32),
            pltpu.VMEM((nz, SUB, half), F32),
            pltpu.VMEM((SUB, half), BF16),
            pltpu.VMEM((2, nz, SUB, half), BF16),
            pltpu.VMEM((halves, n * SUB, rows), BF16),
            pltpu.VMEM((halves, rows, n * SUB), BF16),
            pltpu.VMEM((rows, TB), F32),
            pltpu.VMEM((trait, blocks, q), F32),
            pltpu.VMEM((trait, blocks, q), F32),
            pltpu.VMEM((trait, blocks, q), F32),
            pltpu.VMEM((trait, blocks, q), F32),
            pltpu.VMEM((levels, nodes, nodes), F32),
            pltpu.VMEM((levels, nodes, nodes), F32),
            dma((chunks, halves)),
            dma((chunks,)),
            dma((chunks,)),
            dma((chunks, nz)),
            dma((chunks, nz)),
            dma((chunks, nz)),
            dma((chunks, nz)),
            dma((chunks,)),
            dma((chunks,)),
            dma((trait,)),
            dma((trait,)),
            dma((trait,)),
            dma((trait,)),
        ],
        compiler_params=pltpu.CompilerParams(
            collective_id=0, has_side_effects=True, vmem_limit_bytes=40 << 20
        ),
    )(genotype, targets, membership, node_weight, effect_sizes)
    value = pltpu.with_memory_space_constraint(value, pltpu.VMEM)
    scale = pltpu.with_memory_space_constraint(scale, pltpu.VMEM)
    pieces = 8
    return pl.pallas_call(
        functools.partial(scale_kernel, pieces, min(rows // pieces, 128)),
        name="scale",
        out_shape=jax.ShapeDtypeStruct((rows, cols), F32),
        in_specs=[vmem, vmem],
        out_specs=hbm,
        scratch_shapes=[pltpu.VMEM((rows, cols), F32), dma((pieces,))],
        compiler_params=pltpu.CompilerParams(vmem_limit_bytes=40 << 20),
    )(value, scale)


def solution(mesh):
    n, trait = mesh.shape["snp"], mesh.shape["trait"]
    return jax.shard_map(
        functools.partial(body, n, trait),
        mesh=mesh,
        in_specs=(P(None, "snp"), P("snp", "trait"), P("snp", "trait"), P(), P()),
        out_specs=P("snp", "trait"),
        check_vma=False,
    )
```

```python
import functools

import jax
import jax.numpy as jnp
from jax import lax
from jax.experimental import pallas as pl
from jax.experimental.pallas import tpu as pltpu
from jax.sharding import PartitionSpec as P

TB = 128
SUB = 8
STEP = 0.5
F32 = jnp.float32
BF16 = jnp.bfloat16
LAG = 2
MESH = pl.DeviceIdType.MESH
HIGH = lax.Precision.HIGHEST
NT = (((1,), (1,)), ((), ()))
TN = (((0,), (0,)), ((), ()))


def aligned(x, m):
    return x if isinstance(x, int) else pl.multiple_of(x, m)


def one_hot_rows(rows, samples, per, half):
    r = lax.broadcasted_iota(jnp.int32, (rows, samples), 0)
    n = lax.broadcasted_iota(jnp.int32, (rows, samples), 1)
    slot = lax.shift_right_logical(r, 3)
    line = rows // SUB // 2
    owner = jnp.where(slot < line, 2 * slot, 2 * (slot - line) + 1)
    inner = jnp.bitwise_and(r, 7) - half * per
    hit = (n == owner * per + inner) & (inner >= 0) & (inner < per)
    return jnp.where(hit, 1.0, 0.0).astype(BF16)


def fit_kernel(
    n, trait, chunks, row_tile,
    g_ref, t_ref, m_ref, w_ref, e_hbm,
    v_ref, sc_ref,
    send, near, both, got, res, rg, gs, gt, bq, bt, gq, so, si, ssum, thr,
    e_sem, p_send, p_recv, rs_send, rs_recv, ag_send, ag_recv, b_send, b_recv, x_send, x_recv, y_send, y_recv,
):
    me = lax.axis_index("snp")
    mt = lax.axis_index("trait")
    mp = lax.rem(me, 2)
    mz = me // 2
    nz = n // 2
    samples, rows = g_ref.shape
    per = samples // n
    halves = SUB // per
    cols = v_ref.shape[1]
    half = cols // halves
    w = half // chunks
    blocks = cols // TB
    levels = m_ref.shape[0]
    q = rows // trait

    def col(h, c):
        return pl.ds(aligned(h * half + c * w, w), w)

    def part(c):
        return pl.ds(aligned(c * w, w), w)

    def load(h, c):
        return pltpu.make_async_copy(
            e_hbm.at[:, col(h, c)], v_ref.at[:, col(h, c)], e_sem.at[c, h]
        )

    for c in range(chunks):
        for h in range(halves):
            load(h, c).start()

    barrier = pltpu.get_barrier_semaphore()

    def greet(to):
        pl.semaphore_signal(barrier, inc=1, device_id=to, device_id_type=MESH)

    def greet_snp(k, _):
        greet({"snp": 2 * lax.rem(mz + k, nz) + mp})
        return 0

    def greet_trait(k, _):
        greet({"trait": lax.rem(mt + k, trait)})
        return 0

    greet({"snp": me + 1 - 2 * mp})
    lax.fori_loop(1, nz, greet_snp, 0)
    lax.fori_loop(1, trait, greet_trait, 0)

    for h in range(halves):
        pick = one_hot_rows(n * SUB, samples, per, h)
        gs[h] = jnp.dot(pick, g_ref[...], preferred_element_type=F32).astype(BF16)
        gt[h] = lax.dot_general(
            g_ref[...], pick, (((0,), (1,)), ((), ())), preferred_element_type=F32
        ).astype(BF16)

    for level in range(levels):
        member = m_ref[level].astype(F32)
        count = jnp.sum(member, axis=1, keepdims=True)
        weight = jnp.broadcast_to(w_ref[level : level + 1, :], member.shape).T
        by_node = STEP * weight * jnp.sqrt(TB * jnp.maximum(count, 1.0))
        thr[level] = lax.dot_general(
            member, by_node, TN, precision=HIGH, preferred_element_type=F32
        )
        ssum[level] = lax.dot_general(
            member, member, TN, precision=HIGH, preferred_element_type=F32
        )

    pl.semaphore_wait(barrier, nz + trait - 1)

    def pair_copy(c):
        return pltpu.make_async_remote_copy(
            src_ref=send.at[1 - mp, :, :, part(c)],
            dst_ref=near.at[:, :, part(c)],
            send_sem=p_send.at[c],
            recv_sem=p_recv.at[c],
            device_id={"snp": me + 1 - 2 * mp},
            device_id_type=MESH,
        )

    def rs_copy(c, to, frm):
        return pltpu.make_async_remote_copy(
            src_ref=both.at[to, :, part(c)],
            dst_ref=got.at[frm, :, part(c)],
            send_sem=rs_send.at[c, to],
            recv_sem=rs_recv.at[c, frm],
            device_id={"snp": 2 * to + mp},
            device_id_type=MESH,
        )

    def ag_copy(c, to, frm):
        return pltpu.make_async_remote_copy(
            src_ref=res.at[:, part(c)],
            dst_ref=rg.at[mp, frm, :, part(c)],
            send_sem=ag_send.at[c, to],
            recv_sem=ag_recv.at[c, frm],
            device_id={"snp": 2 * to + mp},
            device_id_type=MESH,
        )

    def back_copy(c, parity):
        return pltpu.make_async_remote_copy(
            src_ref=rg.at[parity, :, :, part(c)],
            dst_ref=rg.at[parity, :, :, part(c)],
            send_sem=b_send.at[c],
            recv_sem=b_recv.at[c],
            device_id={"snp": me + 1 - 2 * mp},
            device_id_type=MESH,
        )

    def x_copy(to, frm):
        return pltpu.make_async_remote_copy(
            src_ref=bt.at[to],
            dst_ref=gq.at[frm],
            send_sem=x_send.at[to],
            recv_sem=x_recv.at[frm],
            device_id={"trait": to},
            device_id_type=MESH,
        )

    def y_copy(to, frm):
        return pltpu.make_async_remote_copy(
            src_ref=so.at[to],
            dst_ref=si.at[frm],
            send_sem=y_send.at[to],
            recv_sem=y_recv.at[frm],
            device_id={"trait": to},
            device_id_type=MESH,
        )

    def peers(count, own, fn):
        def step(k, _):
            fn(lax.rem(own + k, count))
            return 0

        lax.fori_loop(1, count, step, 0)

    kt = min(rows, 256)

    def fit_chunk(c, _):
        total = jnp.zeros((n * SUB, w), F32)
        for h in range(halves):
            load(h, c).wait()
            for k in range(rows // kt):
                total += jnp.dot(
                    gs[h, :, k * kt : (k + 1) * kt],
                    v_ref[k * kt : (k + 1) * kt, col(h, c)].astype(BF16),
                    preferred_element_type=F32,
                )
        send[:, :, :, part(c)] = total.reshape(2, nz, SUB, w)
        pair_copy(c).start()
        return 0

    def pair_chunk(c, _):
        pair_copy(c).wait_recv()
        both[:, :, part(c)] = send[mp, :, :, part(c)] + near[:, :, part(c)]
        peers(nz, mz, lambda p: rs_copy(c, p, mz).start())
        got[mz, :, part(c)] = both[mz, :, part(c)]
        return 0

    for c in range(chunks + LAG):
        if c < chunks:
            fit_chunk(c, 0)
        if c >= LAG:
            pair_chunk(c - LAG, 0)

    def res_chunk(c):
        peers(nz, mz, lambda p: rs_copy(c, p, p).wait_recv())
        fitted = jnp.sum(got[:, :, part(c)], axis=0)
        target = jnp.concatenate(
            [t_ref[:, col(h, c)].astype(F32) for h in range(halves)], axis=0
        )
        residual = (target - fitted).astype(BF16)
        res[:, part(c)] = residual
        rg[mp, mz, :, part(c)] = residual
        peers(nz, mz, lambda p: ag_copy(c, p, mz).start())

    def back_chunk(c):
        peers(nz, mz, lambda p: ag_copy(c, p, p).wait_recv())
        back_copy(c, mp).start()

    lane = lax.broadcasted_iota(jnp.int32, (row_tile, TB), 1)

    def value_chunk(c, _):
        back_copy(c, 1 - mp).wait_recv()
        resid = rg[:, :, :, part(c)].reshape(n * SUB, w)

        def tile(i, _):
            r = pl.ds(pl.multiple_of(i * row_tile, row_tile), row_tile)
            sums = bq[r, :]
            for h in range(halves):
                grad = jnp.dot(gt[h, r, :], resid, preferred_element_type=F32)
                value = v_ref[r, col(h, c)] + STEP * grad
                v_ref[r, col(h, c)] = value
                sq = value * value
                first = (h * half + c * w) // TB
                for b in range(w // TB):
                    s = jnp.sum(sq[:, b * TB : (b + 1) * TB], axis=1, keepdims=True)
                    sums = jnp.where(lane == first + b, s, sums)
            bq[r, :] = sums
            return 0

        lax.fori_loop(0, rows // row_tile, tile, 0)
        return 0

    bq[...] = jnp.zeros_like(bq)
    for c in range(chunks + 1):
        if c < chunks:
            res_chunk(c)
        if c >= 1:
            back_chunk(c - 1)
    lax.fori_loop(0, chunks, value_chunk, 0)

    for k in range(trait):
        bt[k] = bq[k * q : (k + 1) * q, :].T[:blocks]
    peers(trait, mt, lambda p: x_copy(p, mt).start())
    gq[mt] = bt[mt]
    peers(trait, mt, lambda p: x_copy(p, p).wait_recv())

    block_sq = gq[...].reshape(trait * blocks, q)
    scale = None
    for level in range(levels):
        if level == 0:
            node_sq = block_sq
        else:
            node_sq = jnp.dot(
                ssum[level], block_sq, precision=HIGH, preferred_element_type=F32
            )
        norm = jnp.sqrt(node_sq)
        limit = thr[level][:, :1]
        factor = jnp.maximum(norm - limit, 0.0) / jnp.maximum(norm, limit)
        scale = factor if scale is None else scale * factor
        block_sq = block_sq * (factor * factor)
    so[...] = scale.reshape(trait, blocks, q)
    peers(trait, mt, lambda p: y_copy(p, mt).start())
    si[mt] = so[mt]
    peers(trait, mt, lambda p: y_copy(p, p).wait_recv())
    for k in range(trait):
        sc_ref[k * q : (k + 1) * q, :blocks] = si[k].T

    def drain(c, _):
        pair_copy(c).wait_send()
        peers(nz, mz, lambda p: rs_copy(c, p, mz).wait_send())
        peers(nz, mz, lambda p: ag_copy(c, p, mz).wait_send())
        back_copy(c, mp).wait_send()
        return 0

    lax.fori_loop(0, chunks, drain, 0)
    peers(trait, mt, lambda p: x_copy(p, mt).wait_send())
    peers(trait, mt, lambda p: y_copy(p, mt).wait_send())


def scale_kernel(pieces, row_tile, v_ref, sc_ref, o_hbm, out, sem):
    rows, cols = v_ref.shape
    size = rows // pieces

    def store(p):
        r = pl.ds(pl.multiple_of(p * size, size), size)
        return pltpu.make_async_copy(out.at[r, :], o_hbm.at[r, :], sem.at[p])

    def piece(p, _):
        def tile(i, _):
            start = pl.multiple_of(p * size + i * row_tile, row_tile)
            r = pl.ds(start, row_tile)
            sc = sc_ref[r, :]
            for b in range(cols // TB):
                c = slice(b * TB, (b + 1) * TB)
                out[r, c] = v_ref[r, c] * sc[:, b : b + 1]
            return 0

        lax.fori_loop(0, size // row_tile, tile, 0)
        store(p).start()
        return 0

    lax.fori_loop(0, pieces, piece, 0)
    lax.fori_loop(0, pieces, lambda p, _: (store(p).wait(), 0)[1], 0)


def body(n, trait, genotype, targets, effect_sizes, membership, node_weight):
    samples, rows = genotype.shape
    cols = effect_sizes.shape[1]
    blocks = cols // TB
    levels, nodes, _ = membership.shape
    halves = SUB // (samples // n)
    half = cols // halves
    chunks = 4
    nz = n // 2
    q = rows // trait
    vmem = pl.BlockSpec(memory_space=pltpu.VMEM)
    hbm = pl.BlockSpec(memory_space=pl.ANY)
    dma = pltpu.SemaphoreType.DMA
    value, scale = pl.pallas_call(
        functools.partial(fit_kernel, n, trait, chunks, min(rows, 512)),
        name="fit",
        out_shape=(pltpu.VMEM((rows, cols), F32), pltpu.VMEM((rows, TB), F32)),
        in_specs=[vmem] * 4 + [hbm],
        out_specs=(vmem, vmem),
        scratch_shapes=[
            pltpu.VMEM((2, nz, SUB, half), F32),
            pltpu.VMEM((nz, SUB, half), F32),
            pltpu.VMEM((nz, SUB, half), F32),
            pltpu.VMEM((nz, SUB, half), F32),
            pltpu.VMEM((SUB, half), BF16),
            pltpu.VMEM((2, nz, SUB, half), BF16),
            pltpu.VMEM((halves, n * SUB, rows), BF16),
            pltpu.VMEM((halves, rows, n * SUB), BF16),
            pltpu.VMEM((rows, TB), F32),
            pltpu.VMEM((trait, blocks, q), F32),
            pltpu.VMEM((trait, blocks, q), F32),
            pltpu.VMEM((trait, blocks, q), F32),
            pltpu.VMEM((trait, blocks, q), F32),
            pltpu.VMEM((levels, nodes, nodes), F32),
            pltpu.VMEM((levels, nodes, nodes), F32),
            dma((chunks, halves)),
            dma((chunks,)),
            dma((chunks,)),
            dma((chunks, nz)),
            dma((chunks, nz)),
            dma((chunks, nz)),
            dma((chunks, nz)),
            dma((chunks,)),
            dma((chunks,)),
            dma((trait,)),
            dma((trait,)),
            dma((trait,)),
            dma((trait,)),
        ],
        compiler_params=pltpu.CompilerParams(
            collective_id=0, has_side_effects=True, vmem_limit_bytes=40 << 20
        ),
    )(genotype, targets, membership, node_weight, effect_sizes)
    value = pltpu.with_memory_space_constraint(value, pltpu.VMEM)
    scale = pltpu.with_memory_space_constraint(scale, pltpu.VMEM)
    pieces = 8
    return pl.pallas_call(
        functools.partial(scale_kernel, pieces, min(rows // pieces, 128)),
        name="scale",
        out_shape=jax.ShapeDtypeStruct((rows, cols), F32),
        in_specs=[vmem, vmem],
        out_specs=hbm,
        scratch_shapes=[pltpu.VMEM((rows, cols), F32), dma((pieces,))],
        compiler_params=pltpu.CompilerParams(vmem_limit_bytes=40 << 20),
    )(value, scale)


def solution(mesh):
    n, trait = mesh.shape["snp"], mesh.shape["trait"]
    return jax.shard_map(
        functools.partial(body, n, trait),
        mesh=mesh,
        in_specs=(P(None, "snp"), P("snp", "trait"), P("snp", "trait"), P(), P()),
        out_specs=P("snp", "trait"),
        check_vma=False,
    )
```
